32 devices in a mesh: lon: 8 (over z, core), lat: 4 (over y, x).
Axes of the slice: x: 2, y: 2, z: 4, core: 2. Of those that a mesh axis runs over, the one named last changes fastest.
Arguments:
- head: float32 [4, 256, 16384], P(None, 'lat', 'lon'), may hold values from -6 to 6
- storage: float32 [4, 256, 16384], P(None, 'lat', 'lon'), may hold values from 0.5 to 2
- east_cond: float32 [4, 256, 16384], P(None, 'lat', 'lon'), may hold values from 0.1 to 1
- north_cond: float32 [4, 256, 16384], P(None, 'lat', 'lon'), may hold values from 0.1 to 1
- leakance: float32 [3, 256, 16384], P(None, 'lat', 'lon'), may hold values from 0.1 to 1
- recharge: float32 [4, 256, 16384], P(None, 'lat', 'lon'), may hold values from -12 to 12
- recoverable_skeleton_coefs: float32 [3, 256, 16384], P(None, 'lat', 'lon'), may hold values from 0.5 to 2
- permanent_skeleton_coefs: float32 [3, 256, 16384], P(None, 'lat', 'lon'), may hold values from 1 to 4
- critical_heads: float32 [3, 256, 16384], P(None, 'lat', 'lon'), may hold values from -4 to 4
- kernel: float32 [3, 1024], replicated, may hold values from -0.109375 to 0.109375
- land_tiles: int32 [4, 256], P('lat', 'lon'), may hold values 0 or 1
- cell_flags: int32 [4, 256, 16384], P(None, 'lat', 'lon'), may hold values 0 or 1
Outputs:
- new_head: float32 [4, 256, 16384], P(None, 'lat', 'lon')
- new_precon: float32 [3, 256, 16384], P(None, 'lat', 'lon')
- displacement: float32 [256, 16384], P('lat', 'lon')
The draws below stay inside these ranges and needn't reach their ends.
All inputs are finite; a program needn't handle non-finite values. No bound on the sum of `land_tiles` or of `cell_flags` on one device may be relied on, other than what follows from the above.
Results may differ from the reference program's by a relative error of at most 0.0003.
Values sent between devices are 32-bit elements; how exact they have to be, the bound alone decides.
A program may use at most 192 MiB of HBM per device.

```python
import math
import jax
import jax.numpy as jnp

NL = 4
NB = 3
ITERS = 2
TILE = 64
KW = 1024
NLAT = 256
NLON = 16384


def draw_recharge(key, part):
    base = jax.random.normal(key, (NL, NLAT, NLON), jnp.float32)
    rising = 1.0 + 2.0 * jnp.arange(NLAT, dtype=jnp.float32) / max(NLAT - 1, 1)
    return jnp.clip(base, -4.0, 4.0) * rising[None, :, None]


def plant(drawn, rng, low, top_value):
    longest = drawn.shape.index(max(drawn.shape))
    spots = []
    for shift in (0, 1):
        where = [jax.random.randint(jax.random.fold_in(rng, axis), (), 0, length) for axis, length in enumerate(drawn.shape)]
        where[longest] = (where[longest] + shift) % drawn.shape[longest]
        spots.append(tuple(where))
    return drawn.at[spots[0]].set(low).at[spots[1]].set(top_value)


def block_scale(own_key, shape, shards, low, high):
    factor_of, own = 1.0, jax.random.fold_in(own_key, 6)
    for dim, blocks in shards:
        heights = jnp.exp(jax.random.uniform(jax.random.fold_in(own, dim), (blocks,), jnp.float32, low / len(shards), high / len(shards)))
        factor_of = factor_of * jnp.repeat(heights, shape[dim] // blocks).reshape([-1 if axis == dim else 1 for axis in range(len(shape))])
    return factor_of


def scatter_about(stream_key, shape, scale, limit, split=(), held_as=jnp.bfloat16):
    array = jax.random.normal(stream_key, shape, jnp.float32) * scale
    if len(split) > 0:
        array = block_scale(stream_key, shape, split, -0.22, 0.18) * array
    return jnp.clip(array, min=-limit, max=limit).astype(held_as)


def setup_inputs(seed: int = 0) -> dict:
    key_list = jax.random.split(jax.random.key(seed), 13)
    return {
        "head": scatter_about(key_list[0], (NL, NLAT, NLON), 1.0, 6.0, ((1, 4), (2, 8)), jnp.float32),
        "storage": jnp.clip(jnp.exp(math.log(2.0) - 1.3862944 * jax.random.uniform(key_list[1], (NL, NLAT, NLON), jnp.float32) ** block_scale(key_list[1], (NL, NLAT, NLON), ((1, 4), (2, 8)), -0.2, 0.2)), 0.5, 2.0),
        "east_cond": jnp.clip(jnp.exp(math.log(1.0) - 2.3025851 * jax.random.uniform(key_list[2], (NL, NLAT, NLON), jnp.float32) ** block_scale(key_list[2], (NL, NLAT, NLON), ((1, 4), (2, 8)), -0.2, 0.2)), 0.1, 1.0),
        "north_cond": jnp.clip(jnp.exp(math.log(1.0) - 2.3025851 * jax.random.uniform(key_list[3], (NL, NLAT, NLON), jnp.float32) ** block_scale(key_list[3], (NL, NLAT, NLON), ((1, 4), (2, 8)), -0.2, 0.2)), 0.1, 1.0),
        "leakance": jnp.clip(jnp.exp(math.log(1.0) - 2.3025851 * jax.random.uniform(key_list[4], (NB, NLAT, NLON), jnp.float32) ** block_scale(key_list[4], (NB, NLAT, NLON), ((1, 4), (2, 8)), -0.2, 0.2)), 0.1, 1.0),
        "recharge": draw_recharge(jax.random.fold_in(key_list[12], 71), 0),
        "recoverable_skeleton_coefs": jnp.clip(jnp.exp(math.log(2.0) - 1.3862944 * jax.random.uniform(key_list[6], (NB, NLAT, NLON), jnp.float32) ** block_scale(key_list[6], (NB, NLAT, NLON), ((1, 4), (2, 8)), -0.2, 0.2)), 0.5, 2.0),
        "permanent_skeleton_coefs": jnp.clip(jnp.exp(math.log(4.0) - 1.3862944 * jax.random.uniform(key_list[7], (NB, NLAT, NLON), jnp.float32) ** block_scale(key_list[7], (NB, NLAT, NLON), ((1, 4), (2, 8)), -0.2, 0.2)), 1.0, 4.0),
        "critical_heads": scatter_about(key_list[8], (NB, NLAT, NLON), 1.0, 4.0, ((1, 4), (2, 8)), jnp.float32),
        "kernel": scatter_about(key_list[9], (NB, KW), (3 * KW) ** -0.5, 0.109375, (), jnp.float32),
        "land_tiles": plant((jax.random.randint(key_list[10], (NLAT // TILE, NLON // TILE), 0, 4) < 3).astype(jnp.int32), jax.random.fold_in(key_list[10], 1), 0, 1),
        "cell_flags": plant((jax.random.randint(key_list[11], (NL, NLAT, NLON), 0, 16) < 15).astype(jnp.int32), jax.random.fold_in(key_list[11], 1), 0, 1),
    }


def expand_tiles(land_tiles):
    rows, cols = land_tiles.shape
    spread = jnp.broadcast_to(land_tiles[:, None, :, None], (rows, TILE, cols, TILE))
    return spread.reshape(rows * TILE, cols * TILE).astype(jnp.float32)


def reference(head, storage, east_cond, north_cond, leakance, recharge, recoverable_skeleton_coefs, permanent_skeleton_coefs, critical_heads, kernel, land_tiles, cell_flags):
    active = expand_tiles(land_tiles)[None] * cell_flags.astype(jnp.float32)
    west_cond = jnp.roll(east_cond, 1, axis=2)
    south_cond = jnp.concatenate([jnp.zeros((NL, 1, NLON), jnp.float32), north_cond[:, :-1]], axis=1)
    zero_plane = jnp.zeros((1, NLAT, NLON), jnp.float32)
    leak_up = jnp.concatenate([leakance, zero_plane], axis=0)
    leak_down = jnp.concatenate([zero_plane, leakance], axis=0)
    diagonal = storage + east_cond + west_cond + north_cond + south_cond + leak_up + leak_down

    def apply_op(field):
        masked = active * field
        east_val = jnp.roll(masked, -1, axis=2)
        west_val = jnp.roll(masked, 1, axis=2)
        padded_field = jnp.pad(masked, ((0, 0), (1, 1), (0, 0)))
        north_val = padded_field[:, 2:]
        south_val = padded_field[:, :-2]
        upper_val = jnp.concatenate([masked[1:], zero_plane], axis=0)
        lower_val = jnp.concatenate([zero_plane, masked[:-1]], axis=0)
        beside = east_cond * east_val + west_cond * west_val + north_cond * north_val + south_cond * south_val
        beside = beside + leak_up * upper_val + leak_down * lower_val
        return active * (diagonal * masked - beside) + (1.0 - active) * field

    right = active * (storage * head + recharge) + (1.0 - active) * head
    solution = head
    residual = right - apply_op(head)
    direction = residual
    norm_now = jnp.sum(residual * residual)
    for step in range(ITERS):
        image = apply_op(direction)
        alpha = norm_now / jnp.sum(direction * image)
        solution = solution + alpha * direction
        residual = residual - alpha * image
        norm_next = jnp.sum(residual * residual)
        direction = residual + (norm_next / norm_now) * direction
        norm_now = norm_next
    paired_portions = active[:-1] * active[1:]
    prior_centre_heads = 0.5 * (head[:-1] + head[1:])
    renewed_centre_heads = 0.5 * (solution[:-1] + solution[1:])
    clay_lens_subsidence = paired_portions * (recoverable_skeleton_coefs * (prior_centre_heads - renewed_centre_heads) + permanent_skeleton_coefs * (jax.nn.relu(critical_heads - renewed_centre_heads) - jax.nn.relu(critical_heads - prior_centre_heads)))
    new_precon = critical_heads - paired_portions * jax.nn.relu(critical_heads - renewed_centre_heads)
    offsets = (KW // 2 - jnp.arange(KW, dtype=jnp.int32)) % NLON
    wrapped_grid_map = jnp.zeros((NB, NLON), jnp.float32).at[:, offsets].set(kernel)
    fourier_coefs = jnp.fft.rfft(clay_lens_subsidence, axis=2) * jnp.fft.rfft(wrapped_grid_map, axis=1)[:, None, :]
    displacement = jnp.sum(jnp.fft.irfft(fourier_coefs, n=NLON, axis=2), axis=0).astype(jnp.float32)
    return solution, new_precon, displacement
```

```python
import functools

import jax
import jax.numpy as jnp
from jax import lax
from jax.experimental import pallas as pl
from jax.experimental.pallas import tpu as pltpu
from jax.sharding import PartitionSpec as P

MESH = pl.DeviceIdType.MESH
BLOCK = 256


def kernel(
    nlon, nlat,
    head, stor, east, north, leak, rech, rec, perm, crit, flags, ker, land,
    xo, po, do,
    HB, FL, S, E, N, K, Q, RC, PM, CR, M, U, R, W, FB, TH, TL, CH, CL, OUT, RX, DISP,
    scol, rcol, srow, rrow, snc, rnc, redA, redB,
    insem, outsem, hsend, hrecv, asend, arecv, bsend, brecv, dsend, drecv,
):
    L, rows, cols = HB.shape
    B = L - 1
    bands = rows // 8
    tile = cols // land.shape[1]
    width = ker.shape[1]
    lon, lat = lax.axis_index("lon"), lax.axis_index("lat")
    eastd = lax.rem(lon + 1, nlon)
    westd = lax.rem(lon + nlon - 1, nlon)
    northd = lax.rem(lat + 1, nlat)
    southd = lax.rem(lat + nlat - 1, nlat)
    mid = slice(128, 128 + cols)

    loads = [
        (head, HB), (flags, FL), (east, E.at[:, :, mid]), (north, N), (leak, K), (rech, Q),
        (stor, S), (rec, RC), (perm, PM), (crit, CR),
    ]
    loads = [pltpu.make_async_copy(a, b, insem.at[i]) for i, (a, b) in enumerate(loads)]
    for c in loads:
        c.start()

    barrier = pltpu.get_barrier_semaphore()
    for o in range(1, nlon):
        pl.semaphore_signal(barrier, inc=1, device_id={"lon": lax.rem(lon + o, nlon), "lat": lat}, device_id_type=MESH)
    for o in range(1, nlat):
        pl.semaphore_signal(barrier, inc=1, device_id={"lon": lon, "lat": lax.rem(lat + o, nlat)}, device_id_type=MESH)
    pl.semaphore_wait(barrier, nlon - 1 + nlat - 1)

    sub = lax.broadcasted_iota(jnp.int32, (8, cols), 0)
    lane = lax.broadcasted_iota(jnp.int32, (rows, 128), 1)
    lane1 = lax.broadcasted_iota(jnp.int32, (1, 128), 1)

    spread = (
        lax.broadcasted_iota(jnp.int32, (land.shape[1], cols), 1) // tile
        == lax.broadcasted_iota(jnp.int32, (land.shape[1], cols), 0)
    )
    land_row = jnp.dot(
        jnp.broadcast_to(land[...].astype(jnp.float32), (8, land.shape[1])),
        spread.astype(jnp.float32),
        preferred_element_type=jnp.float32,
    )

    def band(k):
        return pl.ds(pl.multiple_of(k * 8, 8), 8)

    loads[0].wait()
    loads[1].wait()

    @pl.loop(0, bands)
    def _(k):
        for l in range(L):
            m = land_row * FL[l, band(k), :].astype(jnp.float32)
            M[l, band(k), :] = m
            U[l, band(k), mid] = m * HB[l, band(k), :]

    def halo_copies(t):
        routes = [
            (scol.at[t, 0], rcol.at[t, 0], {"lon": eastd, "lat": lat}),
            (scol.at[t, 1], rcol.at[t, 1], {"lon": westd, "lat": lat}),
            (srow.at[t, 0], rrow.at[t, 0], {"lon": lon, "lat": northd}),
            (srow.at[t, 1], rrow.at[t, 1], {"lon": lon, "lat": southd}),
        ]
        if t == 0:
            routes.append((snc, rnc, {"lon": lon, "lat": northd}))
        return [
            pltpu.make_async_remote_copy(
                src_ref=s, dst_ref=d, send_sem=hsend.at[t, i], recv_sem=hrecv.at[t, i],
                device_id=to, device_id_type=MESH,
            )
            for i, (s, d, to) in enumerate(routes)
        ]

    def pack(t, ref):
        last = jnp.zeros((rows, 128), jnp.float32)
        first = jnp.zeros((rows, 128), jnp.float32)
        for l in range(L):
            tail = ref[l, 0:rows, cols:cols + 128]
            last = jnp.where(lane == l, pltpu.roll(tail, (l + 1) % 128, 1), last)
            start = ref[l, 0:rows, 128:256]
            first = jnp.where(lane == l, start if l == 0 else pltpu.roll(start, l, 1), first)
            srow[t, 0, l:l + 1, :] = ref[l, rows - 8:rows, mid][7:8, :]
            srow[t, 1, l:l + 1, :] = ref[l, 0:8, mid][0:1, :]
            if t == 0:
                tail = E[l, :, cols:cols + 128]
                last = jnp.where(lane == L + l, pltpu.roll(tail, (L + l + 1) % 128, 1), last)
                snc[l:l + 1, :] = N[l, rows - 8:rows, :][7:8, :]
        scol[t, 0] = last
        scol[t, 1] = first

    def send_halo(t, ref):
        pack(t, ref)
        copies = halo_copies(t)
        for c in copies:
            c.start()
        return copies

    has_south = (lat > 0).astype(jnp.float32)
    has_north = (lat < nlat - 1).astype(jnp.float32)

    def take_halo(t, ref, copies):
        for c in copies:
            c.wait()
        if t == 0:
            for l in range(L):
                E[l, :, 0:128] = jnp.broadcast_to(rcol[0, 0][:, L + l:L + l + 1], (rows, 128))
        for l in range(L):
            ref[l, 0:rows, 0:128] = jnp.broadcast_to(rcol[t, 0][:, l:l + 1], (rows, 128))
            ref[l, 0:rows, cols + 128:cols + 256] = jnp.broadcast_to(rcol[t, 1][:, l:l + 1], (rows, 128))
            ref[l, rows:rows + 8, mid] = jnp.broadcast_to(rrow[t, 1, l:l + 1, :] * has_north, (8, cols))
            below = (rnc[l:l + 1, :] * has_south) * (rrow[t, 0, l:l + 1, :] - ref[l, 0:8, mid][0:1, :])
            FB[l] = jnp.broadcast_to(below, (8, cols))

    def divergence(ref, k):
        centre, out = [], []
        for l in range(L):
            u = ref[l, band(k), :]
            e = E[l, band(k), :]
            ue = pltpu.roll(u, cols + 255, 1)
            fe = e * (u[:, :cols + 128] - ue[:, :cols + 128])
            acc = fe[:, 128:] - pltpu.roll(fe, 1, 1)[:, 128:]
            uc = u[:, mid]
            nxt = ref[l, band(k + 1), mid]
            un = jnp.where(sub == 7, pltpu.roll(nxt, 7, 0), pltpu.roll(uc, 7, 0))
            fn = N[l, band(k), :] * (uc - un)
            rf = pltpu.roll(fn, 1, 0)
            acc = acc + fn - jnp.where(sub == 0, FB[l], rf)
            FB[l] = rf
            if l > 0:
                fv = K[l - 1, band(k), :] * (centre[l - 1] - uc)
                out[l - 1] = out[l - 1] + fv
                acc = acc - fv
            centre.append(uc)
            out.append(acc)
        return centre, out

    def fold(v):
        total = v[:, 0:128]
        for c in range(128, cols, 128):
            total = total + v[:, c:c + 128]
        return total

    def all_reduce(t, va, vb):
        a = jnp.sum(va, axis=0, keepdims=True)
        b = jnp.sum(vb, axis=0, keepdims=True)
        v = jnp.where(lane1 < 64, a + pltpu.roll(a, 64, 1), b + pltpu.roll(b, 64, 1))
        redA[t, lon] = v

        def lon_copy(o):
            return pltpu.make_async_remote_copy(
                src_ref=redA.at[t, lon], dst_ref=redA.at[t, lon], send_sem=asend.at[t, o], recv_sem=arecv.at[t, o],
                device_id={"lon": lax.rem(lon + o, nlon), "lat": lat}, device_id_type=MESH,
            )

        def lat_copy(o):
            return pltpu.make_async_remote_copy(
                src_ref=redB.at[t, lat], dst_ref=redB.at[t, lat], send_sem=bsend.at[t, o], recv_sem=brecv.at[t, o],
                device_id={"lon": lon, "lat": lax.rem(lat + o, nlat)}, device_id_type=MESH,
            )

        first = [lon_copy(o) for o in range(1, nlon)]
        second = [lat_copy(o) for o in range(1, nlat)]

        def start():
            for c in first:
                c.start()

        def middle():
            for c in first:
                c.wait()
            redB[t, lat] = jnp.sum(redA[t], axis=0)
            for c in second:
                c.start()

        def finish():
            for c in second:
                c.wait()
            total = jnp.sum(redB[t], axis=0)
            a = jnp.sum(jnp.where(lane1 < 64, total, 0.0), axis=1, keepdims=True)
            b = jnp.sum(jnp.where(lane1 < 64, 0.0, total), axis=1, keepdims=True)
            return a, b

        return start, middle, finish

    zero = jnp.zeros((8, 128), jnp.float32)
    loads[2].wait()
    loads[3].wait()
    copies = send_halo(0, U)
    loads[4].wait()
    loads[5].wait()
    take_halo(0, U, copies)

    @pl.loop(0, bands)
    def _(k):
        _, out = divergence(U, k)
        for l in range(L):
            R[l, band(k), mid] = M[l, band(k), :] * (Q[l, band(k), :] - out[l])

    copies = send_halo(1, R)
    loads[6].wait()
    take_halo(1, R, copies)

    def second(k, carry):
        a, b = carry
        centre, out = divergence(R, k)
        for l in range(L):
            r = centre[l]
            w = M[l, band(k), :] * (S[l, band(k), :] * r + out[l])
            W[l, band(k), mid] = w
            a = a + fold(r * r)
            b = b + fold(r * w)
        return a, b

    a, b = lax.fori_loop(0, bands, second, (zero, zero))
    start, middle, finish = all_reduce(0, a, b)
    start()
    copies = send_halo(2, W)
    take_halo(2, W, copies)
    middle()

    @pl.loop(0, bands)
    def _(k):
        centre, out = divergence(W, k)
        for l in range(L):
            Q[l, band(k), :] = M[l, band(k), :] * (S[l, band(k), :] * centre[l] + out[l])

    rr0, bend = finish()
    alpha0 = rr0 / bend
    alpha_row = jnp.broadcast_to(alpha0, (8, 128))
    alpha_row = jnp.concatenate([alpha_row] * (cols // 128), axis=1)

    def third(k, carry):
        a, b = carry
        for l in range(L):
            w = W[l, band(k), mid]
            r1 = R[l, band(k), mid] - alpha_row * w
            s1 = w - alpha_row * Q[l, band(k), :]
            a = a + fold(r1 * r1)
            b = b + fold(r1 * s1)
        return a, b

    a, b = lax.fori_loop(0, bands, third, (zero, zero))
    start, middle, finish = all_reduce(1, a, b)
    start()

    half = width // 2
    h = half // BLOCK
    nb = cols // BLOCK
    lags = width // 128
    sides = BLOCK // 128

    def piece(b, e):
        if e < 0 or e >= lags:
            return jnp.zeros((1, 128), jnp.float32)
        return ker[b:b + 1, e * 128:(e + 1) * 128]

    for e in range(-1, lags + 2):
        places = [
            (d, ph, jh) for d in range(-h, h + 1) for ph in range(sides) for jh in range(sides)
            if sides * (d + h) + ph - jh == e
        ]
        for b in range(B):
            if 0 <= e <= lags:
                base = jnp.concatenate([piece(b, e), piece(b, e - 1)], axis=1)
                wide = pltpu.roll(jnp.broadcast_to(base, (128, 256)), 0, 1, stride=1, stride_axis=0)
                block = wide[:, :128].T
            else:
                block = jnp.zeros((128, 128), jnp.float32)
            hi = block.astype(jnp.bfloat16)
            lo = (block - hi.astype(jnp.float32)).astype(jnp.bfloat16)
            for d, ph, jh in places:
                at = (d + h, slice(b * BLOCK + ph * 128, b * BLOCK + ph * 128 + 128), slice(jh * 128, jh * 128 + 128))
                TH[at] = hi
                TL[at] = lo

    for i in (7, 8, 9):
        loads[i].wait()
    middle()
    rr1, curve = finish()
    beta = rr1 / rr0
    alpha1 = rr1 / (curve - beta * rr1 / alpha0)
    of_r = jnp.broadcast_to(alpha0 + alpha1 + alpha1 * beta, (16, BLOCK))
    of_w = jnp.broadcast_to(alpha1 * alpha0, (16, BLOCK))

    @pl.loop(0, rows // 16)
    def _(k):
        r = pl.ds(pl.multiple_of(k * 16, 16), 16)
        for p in range(nb):
            cs = slice(p * BLOCK, (p + 1) * BLOCK)
            ps = slice(128 + p * BLOCK, 128 + (p + 1) * BLOCK)
            old = [HB[l, r, cs] for l in range(L)]
            new = [old[l] + of_r * R[l, r, ps] - of_w * W[l, r, ps] for l in range(L)]
            for l in range(L):
                HB[l, r, cs] = new[l]
            for b in range(B):
                both = M[b, r, cs] * M[b + 1, r, cs]
                om = 0.5 * (old[b] + old[b + 1])
                nm = 0.5 * (new[b] + new[b + 1])
                cr = CR[b, r, cs]
                over = jnp.maximum(cr - nm, 0.0)
                comp = both * (RC[b, r, cs] * (om - nm) + PM[b, r, cs] * (over - jnp.maximum(cr - om, 0.0)))
                CR[b, r, cs] = cr - both * over
                hi = comp.astype(jnp.bfloat16)
                lo = (comp - hi.astype(jnp.float32)).astype(jnp.bfloat16)
                dst = pl.ds(pl.multiple_of(p * rows + k * 16, 16), 16)
                CH[dst, b * BLOCK:(b + 1) * BLOCK] = hi
                CL[dst, b * BLOCK:(b + 1) * BLOCK] = lo

    outs = [pltpu.make_async_copy(HB, xo, outsem.at[0]), pltpu.make_async_copy(CR, po, outsem.at[1])]
    for c in outs:
        c.start()

    def product(d, low, high):
        ch, cl = CH[low * rows:high * rows, :], CL[low * rows:high * rows, :]
        th, tl = TH[d + h], TL[d + h]
        dot = functools.partial(jnp.dot, preferred_element_type=jnp.float32)
        return dot(ch, th) + (dot(ch, tl) + dot(cl, th))

    for d in range(h, 0, -1):
        left = product(d, 0, d)
        right = product(-d, nb - d, nb)
        at = slice((h - d) * rows, h * rows)
        end = slice((h + nb) * rows, (h + nb + d) * rows)
        if d == h:
            OUT[at, :] = left
            OUT[end, :] = right
        else:
            OUT[at, :] += left
            OUT[end, :] += right
    exts = [
        pltpu.make_async_remote_copy(
            src_ref=OUT.at[0:h * rows, :], dst_ref=RX.at[1], send_sem=dsend.at[0], recv_sem=drecv.at[0],
            device_id={"lon": westd, "lat": lat}, device_id_type=MESH,
        ),
        pltpu.make_async_remote_copy(
            src_ref=OUT.at[(h + nb) * rows:(2 * h + nb) * rows, :], dst_ref=RX.at[0], send_sem=dsend.at[1], recv_sem=drecv.at[1],
            device_id={"lon": eastd, "lat": lat}, device_id_type=MESH,
        ),
    ]
    for c in exts:
        c.start()
    OUT[h * rows:(h + nb) * rows, :] = product(0, 0, nb)
    for d in range(1, h + 1):
        OUT[h * rows:(h + nb - d) * rows, :] += product(d, d, nb)
        OUT[(h + d) * rows:(h + nb) * rows, :] += product(-d, 0, nb - d)
    for c in exts:
        c.wait()
    for p in range(nb):
        v = OUT[(h + p) * rows:(h + p + 1) * rows, :]
        if p < h:
            v = v + RX[0, p * rows:(p + 1) * rows, :]
        if p >= nb - h:
            q = p - (nb - h)
            v = v + RX[1, q * rows:(q + 1) * rows, :]
        DISP[:, p * BLOCK:(p + 1) * BLOCK] = v
    outs.append(pltpu.make_async_copy(DISP, do, outsem.at[2]))
    outs[2].start()
    for c in outs:
        c.wait()


def per_device(
    nlon, nlat, head, storage, east_cond, north_cond, leakance, recharge,
    recoverable_skeleton_coefs, permanent_skeleton_coefs, critical_heads, kernel_, land_tiles, cell_flags,
):
    L, rows, cols = head.shape
    B = L - 1
    width = kernel_.shape[1]
    f32 = jnp.float32
    full, inter = (L, rows, cols), (B, rows, cols)
    padded = (L, rows + 8, cols + 256)
    h = width // 2 // BLOCK
    nb = cols // BLOCK
    V = pltpu.VMEM
    dma = pltpu.SemaphoreType.DMA
    scratch = [
        V(full, f32), V(full, jnp.int32), V(full, f32), V((L, rows, cols + 128), f32), V(full, f32), V(inter, f32),
        V(full, f32), V(inter, f32), V(inter, f32), V(inter, f32), V(full, f32),
        V(padded, f32), V(padded, f32), V(padded, f32), V((L, 8, cols), f32),
        V((2 * h + 1, B * BLOCK, BLOCK), jnp.bfloat16), V((2 * h + 1, B * BLOCK, BLOCK), jnp.bfloat16),
        V((nb * rows, B * BLOCK), jnp.bfloat16), V((nb * rows, B * BLOCK), jnp.bfloat16),
        V(((nb + 2 * h) * rows, BLOCK), f32), V((2, h * rows, BLOCK), f32), V((rows, cols), f32),
        V((3, 2, rows, 128), f32), V((3, 2, rows, 128), f32),
        V((3, 2, L, cols), f32), V((3, 2, L, cols), f32), V((L, cols), f32), V((L, cols), f32),
        V((2, nlon, 1, 128), f32), V((2, nlat, 1, 128), f32),
        dma((10,)), dma((3,)), dma((3, 5)), dma((3, 5)), dma((2, nlon)), dma((2, nlon)), dma((2, nlat)), dma((2, nlat)),
        dma((2,)), dma((2,)),
    ]
    hbm = pl.BlockSpec(memory_space=pl.ANY)
    vmem = pl.BlockSpec(memory_space=pltpu.VMEM)
    return pl.pallas_call(
        functools.partial(kernel, nlon, nlat),
        out_shape=(
            jax.ShapeDtypeStruct(full, f32), jax.ShapeDtypeStruct(inter, f32), jax.ShapeDtypeStruct((rows, cols), f32),
        ),
        in_specs=[hbm] * 10 + [vmem] * 2,
        out_specs=(hbm,) * 3,
        scratch_shapes=scratch,
        name="aquifer_step",
        compiler_params=pltpu.CompilerParams(collective_id=0, has_side_effects=True, vmem_limit_bytes=60 * 1024 * 1024),
    )(
        head, storage, east_cond, north_cond, leakance, recharge, recoverable_skeleton_coefs,
        permanent_skeleton_coefs, critical_heads, cell_flags, kernel_, land_tiles,
    )


def solution(mesh):
    block = P(None, "lat", "lon")
    placed = (block,) * 9 + (P(), P("lat", "lon"), block)
    return jax.shard_map(
        functools.partial(per_device, mesh.shape["lon"], mesh.shape["lat"]),
        mesh=mesh,
        in_specs=placed,
        out_specs=(block, block, P("lat", "lon")),
        check_vma=False,
    )
```

```python
import functools

import jax
import jax.numpy as jnp
from jax import lax
from jax.experimental import pallas as pl
from jax.experimental.pallas import tpu as pltpu
from jax.sharding import PartitionSpec as P

MESH = pl.DeviceIdType.MESH
BLOCK = 256
GROUPS = 4


def kernel(
    nlon, nlat,
    head, stor, east, north, leak, rech, rec, perm, crit, flags, ker, land,
    xo, po, do,
    HB, FL, S, E, N, K, Q, RC, PM, CR, M, U, R, W, FB, TH, TL, CH, CL, OUT, RX, DISP,
    scol, rcol, srow, rrow, snc, rnc, redA, redB,
    insem, outsem, hsend, hrecv, asend, arecv, bsend, brecv, dsend, drecv,
):
    L, rows, cols = HB.shape
    B = L - 1
    bands = rows // 8
    tile = cols // land.shape[1]
    width = ker.shape[1]
    lon, lat = lax.axis_index("lon"), lax.axis_index("lat")
    eastd = lax.rem(lon + 1, nlon)
    westd = lax.rem(lon + nlon - 1, nlon)
    northd = lax.rem(lat + 1, nlat)
    southd = lax.rem(lat + nlat - 1, nlat)
    mid = slice(128, 128 + cols)

    def fetch(sem, a, b):
        copy = pltpu.make_async_copy(a, b, insem.at[sem])
        copy.start()
        return copy

    group = rows // GROUPS
    early = [fetch(i, a, b) for i, (a, b) in enumerate(((head, HB), (flags, FL), (east, E.at[:, :, mid]), (north, N)))]
    grouped = []
    for g in range(GROUPS):
        rs = slice(g * group, (g + 1) * group)
        grouped.append([fetch(4 + 2 * g, leak.at[:, rs], K.at[:, rs]), fetch(5 + 2 * g, rech.at[:, rs], Q.at[:, rs])])
    late = [
        fetch(4 + 2 * GROUPS + i, a, b) for i, (a, b) in enumerate(((stor, S), (rec, RC), (perm, PM), (crit, CR)))
    ]

    barrier = pltpu.get_barrier_semaphore()
    for o in range(1, nlon):
        pl.semaphore_signal(barrier, inc=1, device_id={"lon": lax.rem(lon + o, nlon), "lat": lat}, device_id_type=MESH)
    for o in range(1, nlat):
        pl.semaphore_signal(barrier, inc=1, device_id={"lon": lon, "lat": lax.rem(lat + o, nlat)}, device_id_type=MESH)

    for ref in (U, R, W):
        for l in range(L):
            ref[l, 0:rows, 0:128] = jnp.zeros((rows, 128), jnp.float32)
            ref[l, 0:rows, cols + 128:cols + 256] = jnp.zeros((rows, 128), jnp.float32)
            ref[l, rows:rows + 8, mid] = jnp.zeros((8, cols), jnp.float32)
    for l in range(L):
        E[l, :, 0:128] = jnp.zeros((rows, 128), jnp.float32)

    sub = lax.broadcasted_iota(jnp.int32, (8, cols), 0)
    lane = lax.broadcasted_iota(jnp.int32, (rows, 128), 1)
    lane1 = lax.broadcasted_iota(jnp.int32, (1, 128), 1)

    spread = (
        lax.broadcasted_iota(jnp.int32, (land.shape[1], cols), 1) // tile
        == lax.broadcasted_iota(jnp.int32, (land.shape[1], cols), 0)
    )
    land_row = jnp.dot(
        jnp.broadcast_to(land[...].astype(jnp.float32), (8, land.shape[1])),
        spread.astype(jnp.float32),
        preferred_element_type=jnp.float32,
    )

    zero = jnp.zeros((8, 128), jnp.float32)

    def band(k):
        return pl.ds(pl.multiple_of(k * 8, 8), 8)

    early[0].wait()
    early[1].wait()

    @pl.loop(0, bands)
    def _(k):
        for l in range(L):
            m = land_row * FL[l, band(k), :].astype(jnp.float32)
            M[l, band(k), :] = m
            U[l, band(k), mid] = m * HB[l, band(k), :]

    def halo_copies(t):
        routes = [
            (scol.at[t, 0], rcol.at[t, 0], {"lon": eastd, "lat": lat}),
            (scol.at[t, 1], rcol.at[t, 1], {"lon": westd, "lat": lat}),
            (srow.at[t, 0], rrow.at[t, 0], {"lon": lon, "lat": northd}),
            (srow.at[t, 1], rrow.at[t, 1], {"lon": lon, "lat": southd}),
        ]
        if t == 0:
            routes.append((snc, rnc, {"lon": lon, "lat": northd}))
        return [
            pltpu.make_async_remote_copy(
                src_ref=s, dst_ref=d, send_sem=hsend.at[t, i], recv_sem=hrecv.at[t, i],
                device_id=to, device_id_type=MESH,
            )
            for i, (s, d, to) in enumerate(routes)
        ]

    def pack(t, ref):
        last = jnp.zeros((rows, 128), jnp.float32)
        first = jnp.zeros((rows, 128), jnp.float32)
        for l in range(L):
            tail = ref[l, 0:rows, cols:cols + 128]
            last = jnp.where(lane == l, pltpu.roll(tail, (l + 1) % 128, 1), last)
            start = ref[l, 0:rows, 128:256]
            first = jnp.where(lane == l, start if l == 0 else pltpu.roll(start, l, 1), first)
            srow[t, 0, l:l + 1, :] = ref[l, rows - 8:rows, mid][7:8, :]
            srow[t, 1, l:l + 1, :] = ref[l, 0:8, mid][0:1, :]
            if t == 0:
                tail = E[l, :, cols:cols + 128]
                last = jnp.where(lane == L + l, pltpu.roll(tail, (L + l + 1) % 128, 1), last)
                snc[l:l + 1, :] = N[l, rows - 8:rows, :][7:8, :]
        scol[t, 0] = last
        scol[t, 1] = first

    def send_halo(t, ref):
        pack(t, ref)
        if t == 0:
            pl.semaphore_wait(barrier, nlon - 1 + nlat - 1)
        copies = halo_copies(t)
        for c in copies:
            c.start()
        for l in range(L):
            if t == 0:
                FB[l] = jnp.zeros((8, cols), jnp.float32)
            else:
                FB[l] = -jnp.broadcast_to((rnc[l:l + 1, :] * has_south) * ref[l, 0:8, mid][0:1, :], (8, cols))
        return copies

    has_south = (lat > 0).astype(jnp.float32)
    has_north = (lat < nlat - 1).astype(jnp.float32)

    def take_halo(t, ref, copies, dst, shift, sign):
        for c in copies:
            c.wait()
        dot = jnp.zeros((8, 128), jnp.float32)

        def add(l, rs, c0, n, delta):
            at = (l, rs, slice(c0 + shift, c0 + shift + n))
            dst[at] = dst[at] + sign * (M[l, rs, c0:c0 + n] * delta)
            part = ref[l, rs, 128 + c0:128 + c0 + n] * delta
            total = zero
            for r in range(0, part.shape[0], 8):
                for c in range(0, n, 128):
                    total = total + part[r:r + 8, c:c + 128]
            return total

        whole, last = slice(0, rows), cols - 128
        for l in range(L):
            far = jnp.broadcast_to(rcol[t, 0][:, l:l + 1], (rows, 128))
            if t == 0:
                E[l, :, 0:128] = jnp.broadcast_to(rcol[0, 0][:, L + l:L + l + 1], (rows, 128))
                far = far - ref[l, 0:rows, 128:256]
            dot = dot + add(l, whole, 0, 128, jnp.where(lane == 0, -E[l, :, 0:128] * far, 0.0))
            far = jnp.broadcast_to(rcol[t, 1][:, l:l + 1], (rows, 128))
            dot = dot + add(l, whole, last, 128, jnp.where(lane == 127, -E[l, :, cols:cols + 128] * far, 0.0))
            far = jnp.broadcast_to(rrow[t, 0, l:l + 1, :] * has_south, (8, cols))
            if t == 0:
                far = far - ref[l, 0:8, mid]
            cond = jnp.broadcast_to(rnc[l:l + 1, :] * has_south, (8, cols))
            dot = dot + add(l, slice(0, 8), 0, cols, jnp.where(sub == 0, -cond * far, 0.0))
            far = jnp.broadcast_to(rrow[t, 1, l:l + 1, :] * has_north, (8, cols))
            dot = dot + add(l, slice(rows - 8, rows), 0, cols, jnp.where(sub == 7, -N[l, rows - 8:rows, :] * far, 0.0))
        return dot

    def divergence(ref, k):
        centre, out = [], []
        for l in range(L):
            u = ref[l, band(k), :]
            e = E[l, band(k), :]
            ue = pltpu.roll(u, cols + 255, 1)
            fe = e * (u[:, :cols + 128] - ue[:, :cols + 128])
            acc = fe[:, 128:] - pltpu.roll(fe, 1, 1)[:, 128:]
            uc = u[:, mid]
            nxt = ref[l, band(k + 1), mid]
            un = jnp.where(sub == 7, pltpu.roll(nxt, 7, 0), pltpu.roll(uc, 7, 0))
            fn = N[l, band(k), :] * (uc - un)
            rf = pltpu.roll(fn, 1, 0)
            acc = acc + fn - jnp.where(sub == 0, FB[l], rf)
            FB[l] = rf
            if l > 0:
                fv = K[l - 1, band(k), :] * (centre[l - 1] - uc)
                out[l - 1] = out[l - 1] + fv
                acc = acc - fv
            centre.append(uc)
            out.append(acc)
        return centre, out

    def fold(v):
        total = v[:, 0:128]
        for c in range(128, cols, 128):
            total = total + v[:, c:c + 128]
        return total

    def all_reduce(t, va, vb):
        a = jnp.sum(va, axis=0, keepdims=True)
        b = jnp.sum(vb, axis=0, keepdims=True)
        v = jnp.where(lane1 < 64, a + pltpu.roll(a, 64, 1), b + pltpu.roll(b, 64, 1))
        redA[t, lon] = v

        def lon_copy(o):
            return pltpu.make_async_remote_copy(
                src_ref=redA.at[t, lon], dst_ref=redA.at[t, lon], send_sem=asend.at[t, o], recv_sem=arecv.at[t, o],
                device_id={"lon": lax.rem(lon + o, nlon), "lat": lat}, device_id_type=MESH,
            )

        def lat_copy(o):
            return pltpu.make_async_remote_copy(
                src_ref=redB.at[t, lat], dst_ref=redB.at[t, lat], send_sem=bsend.at[t, o], recv_sem=brecv.at[t, o],
                device_id={"lon": lon, "lat": lax.rem(lat + o, nlat)}, device_id_type=MESH,
            )

        first = [lon_copy(o) for o in range(1, nlon)]
        second = [lat_copy(o) for o in range(1, nlat)]

        def start():
            for c in first:
                c.start()

        def middle():
            for c in first:
                c.wait()
            redB[t, lat] = jnp.sum(redA[t], axis=0)
            for c in second:
                c.start()

        def finish():
            for c in second:
                c.wait()
            total = jnp.sum(redB[t], axis=0)
            a = jnp.sum(jnp.where(lane1 < 64, total, 0.0), axis=1, keepdims=True)
            b = jnp.sum(jnp.where(lane1 < 64, 0.0, total), axis=1, keepdims=True)
            return a, b

        return start, middle, finish

    early[2].wait()
    early[3].wait()
    copies = send_halo(0, U)
    for g in range(GROUPS):
        for c in grouped[g]:
            c.wait()

        @pl.loop(g * bands // GROUPS, (g + 1) * bands // GROUPS)
        def _(k):
            _, out = divergence(U, k)
            for l in range(L):
                R[l, band(k), mid] = M[l, band(k), :] * (Q[l, band(k), :] - out[l])

    take_halo(0, U, copies, R, 128, -1.0)
    copies = send_halo(1, R)
    late[0].wait()

    def second(k, carry):
        a, b = carry
        centre, out = divergence(R, k)
        for l in range(L):
            r = centre[l]
            w = M[l, band(k), :] * (S[l, band(k), :] * r + out[l])
            W[l, band(k), mid] = w
            a = a + fold(r * r)
            b = b + fold(r * w)
        return a, b

    a, b = lax.fori_loop(0, bands, second, (zero, zero))
    b = b + take_halo(1, R, copies, W, 128, 1.0)
    start, middle, finish = all_reduce(0, a, b)
    start()
    copies = send_halo(2, W)

    @pl.loop(0, bands)
    def _(k):
        centre, out = divergence(W, k)
        for l in range(L):
            Q[l, band(k), :] = M[l, band(k), :] * (S[l, band(k), :] * centre[l] + out[l])

    middle()
    take_halo(2, W, copies, Q, 0, 1.0)
    rr0, bend = finish()
    alpha0 = rr0 / bend
    alpha_row = jnp.broadcast_to(alpha0, (8, 128))
    alpha_row = jnp.concatenate([alpha_row] * (cols // 128), axis=1)

    def third(k, carry):
        a, b = carry
        for l in range(L):
            w = W[l, band(k), mid]
            r1 = R[l, band(k), mid] - alpha_row * w
            s1 = w - alpha_row * Q[l, band(k), :]
            a = a + fold(r1 * r1)
            b = b + fold(r1 * s1)
        return a, b

    a, b = lax.fori_loop(0, bands, third, (zero, zero))
    start, middle, finish = all_reduce(1, a, b)
    start()

    half = width // 2
    h = half // BLOCK
    nb = cols // BLOCK
    lags = width // 128
    sides = BLOCK // 128

    def piece(b, e):
        if e < 0 or e >= lags:
            return jnp.zeros((1, 128), jnp.float32)
        return ker[b:b + 1, e * 128:(e + 1) * 128]

    for e in range(-1, lags + 2):
        places = [
            (d, ph, jh) for d in range(-h, h + 1) for ph in range(sides) for jh in range(sides)
            if sides * (d + h) + ph - jh == e
        ]
        for b in range(B):
            if 0 <= e <= lags:
                base = jnp.concatenate([piece(b, e), piece(b, e - 1)], axis=1)
                wide = pltpu.roll(jnp.broadcast_to(base, (128, 256)), 0, 1, stride=1, stride_axis=0)
                block = wide[:, :128].T
            else:
                block = jnp.zeros((128, 128), jnp.float32)
            hi = block.astype(jnp.bfloat16)
            lo = (block - hi.astype(jnp.float32)).astype(jnp.bfloat16)
            for d, ph, jh in places:
                at = (d + h, slice(b * BLOCK + ph * 128, b * BLOCK + ph * 128 + 128), slice(jh * 128, jh * 128 + 128))
                TH[at] = hi
                TL[at] = lo

    for c in late[1:]:
        c.wait()
    middle()
    rr1, curve = finish()
    beta = rr1 / rr0
    alpha1 = rr1 / (curve - beta * rr1 / alpha0)
    of_r = jnp.broadcast_to(alpha0 + alpha1 + alpha1 * beta, (16, BLOCK))
    of_w = jnp.broadcast_to(alpha1 * alpha0, (16, BLOCK))

    def compact(blocks):
        @pl.loop(0, rows // 16)
        def _(k):
            r = pl.ds(pl.multiple_of(k * 16, 16), 16)
            for p in blocks:
                cs = slice(p * BLOCK, (p + 1) * BLOCK)
                ps = slice(128 + p * BLOCK, 128 + (p + 1) * BLOCK)
                old = [HB[l, r, cs] for l in range(L)]
                new = [old[l] + of_r * R[l, r, ps] - of_w * W[l, r, ps] for l in range(L)]
                for l in range(L):
                    xo[l, r, cs] = new[l]
                for b in range(B):
                    both = M[b, r, cs] * M[b + 1, r, cs]
                    om = 0.5 * (old[b] + old[b + 1])
                    nm = 0.5 * (new[b] + new[b + 1])
                    cr = CR[b, r, cs]
                    over = jnp.maximum(cr - nm, 0.0)
                    comp = both * (RC[b, r, cs] * (om - nm) + PM[b, r, cs] * (over - jnp.maximum(cr - om, 0.0)))
                    po[b, r, cs] = cr - both * over
                    hi = comp.astype(jnp.bfloat16)
                    lo = (comp - hi.astype(jnp.float32)).astype(jnp.bfloat16)
                    dst = pl.ds(pl.multiple_of(p * rows + k * 16, 16), 16)
                    CH[dst, b * BLOCK:(b + 1) * BLOCK] = hi
                    CL[dst, b * BLOCK:(b + 1) * BLOCK] = lo

    edge = [p for p in range(nb) if p < h or p >= nb - h]
    compact(edge)

    def product(d, low, high):
        ch, cl = CH[low * rows:high * rows, :], CL[low * rows:high * rows, :]
        th, tl = TH[d + h], TL[d + h]
        dot = functools.partial(jnp.dot, preferred_element_type=jnp.float32)
        return dot(ch, th) + (dot(ch, tl) + dot(cl, th))

    for d in range(h, 0, -1):
        left = product(d, 0, d)
        right = product(-d, nb - d, nb)
        at = slice((h - d) * rows, h * rows)
        end = slice((h + nb) * rows, (h + nb + d) * rows)
        if d == h:
            OUT[at, :] = left
            OUT[end, :] = right
        else:
            OUT[at, :] += left
            OUT[end, :] += right
    exts = [
        pltpu.make_async_remote_copy(
            src_ref=OUT.at[0:h * rows, :], dst_ref=RX.at[1], send_sem=dsend.at[0], recv_sem=drecv.at[0],
            device_id={"lon": westd, "lat": lat}, device_id_type=MESH,
        ),
        pltpu.make_async_remote_copy(
            src_ref=OUT.at[(h + nb) * rows:(2 * h + nb) * rows, :], dst_ref=RX.at[0], send_sem=dsend.at[1], recv_sem=drecv.at[1],
            device_id={"lon": eastd, "lat": lat}, device_id_type=MESH,
        ),
    ]
    for c in exts:
        c.start()
    compact([p for p in range(nb) if p not in edge])
    OUT[h * rows:(h + nb) * rows, :] = product(0, 0, nb)
    for d in range(1, h + 1):
        OUT[h * rows:(h + nb - d) * rows, :] += product(d, d, nb)
        OUT[(h + d) * rows:(h + nb) * rows, :] += product(-d, 0, nb - d)
    for c in exts:
        c.wait()
    for p in range(nb):
        v = OUT[(h + p) * rows:(h + p + 1) * rows, :]
        if p < h:
            v = v + RX[0, p * rows:(p + 1) * rows, :]
        if p >= nb - h:
            q = p - (nb - h)
            v = v + RX[1, q * rows:(q + 1) * rows, :]
        do[:, p * BLOCK:(p + 1) * BLOCK] = v


def per_device(
    nlon, nlat, head, storage, east_cond, north_cond, leakance, recharge,
    recoverable_skeleton_coefs, permanent_skeleton_coefs, critical_heads, kernel_, land_tiles, cell_flags,
):
    L, rows, cols = head.shape
    B = L - 1
    width = kernel_.shape[1]
    f32 = jnp.float32
    full, inter = (L, rows, cols), (B, rows, cols)
    padded = (L, rows + 8, cols + 256)
    h = width // 2 // BLOCK
    nb = cols // BLOCK
    V = pltpu.VMEM
    dma = pltpu.SemaphoreType.DMA
    scratch = [
        V(full, f32), V(full, jnp.int32), V(full, f32), V((L, rows, cols + 128), f32), V(full, f32), V(inter, f32),
        V(full, f32), V(inter, f32), V(inter, f32), V(inter, f32), V(full, f32),
        V(padded, f32), V(padded, f32), V(padded, f32), V((L, 8, cols), f32),
        V((2 * h + 1, B * BLOCK, BLOCK), jnp.bfloat16), V((2 * h + 1, B * BLOCK, BLOCK), jnp.bfloat16),
        V((nb * rows, B * BLOCK), jnp.bfloat16), V((nb * rows, B * BLOCK), jnp.bfloat16),
        V(((nb + 2 * h) * rows, BLOCK), f32), V((2, h * rows, BLOCK), f32), V((rows, cols), f32),
        V((3, 2, rows, 128), f32), V((3, 2, rows, 128), f32),
        V((3, 2, L, cols), f32), V((3, 2, L, cols), f32), V((L, cols), f32), V((L, cols), f32),
        V((2, nlon, 1, 128), f32), V((2, nlat, 1, 128), f32),
        dma((8 + 2 * GROUPS,)), dma((3,)), dma((3, 5)), dma((3, 5)), dma((2, nlon)), dma((2, nlon)), dma((2, nlat)), dma((2, nlat)),
        dma((2,)), dma((2,)),
    ]
    hbm = pl.BlockSpec(memory_space=pl.ANY)
    vmem = pl.BlockSpec(memory_space=pltpu.VMEM)
    outs = pl.pallas_call(
        functools.partial(kernel, nlon, nlat),
        out_shape=(
            V(full, f32), V(inter, f32), V((rows, cols), f32),
        ),
        in_specs=[hbm] * 10 + [vmem] * 2,
        out_specs=(vmem,) * 3,
        scratch_shapes=scratch,
        name="aquifer_step",
        compiler_params=pltpu.CompilerParams(collective_id=0, has_side_effects=True, vmem_limit_bytes=52 * 1024 * 1024),
    )(
        head, storage, east_cond, north_cond, leakance, recharge, recoverable_skeleton_coefs,
        permanent_skeleton_coefs, critical_heads, cell_flags, kernel_, land_tiles,
    )

    def put(a, b, c, x, y, z, sem):
        copies = [pltpu.make_async_copy(s, d, sem.at[i]) for i, (s, d) in enumerate(((a, x), (b, y), (c, z)))]
        for copy in copies:
            copy.start()
        for copy in copies:
            copy.wait()

    return pl.pallas_call(
        put,
        out_shape=(
            jax.ShapeDtypeStruct(full, f32), jax.ShapeDtypeStruct(inter, f32), jax.ShapeDtypeStruct((rows, cols), f32),
        ),
        in_specs=[vmem] * 3,
        out_specs=(hbm,) * 3,
        scratch_shapes=[dma((3,))],
        name="put",
        compiler_params=pltpu.CompilerParams(vmem_limit_bytes=1024 * 1024),
    )(*outs)


def solution(mesh):
    block = P(None, "lat", "lon")
    placed = (block,) * 9 + (P(), P("lat", "lon"), block)
    return jax.shard_map(
        functools.partial(per_device, mesh.shape["lon"], mesh.shape["lat"]),
        mesh=mesh,
        in_specs=placed,
        out_specs=(block, block, P("lat", "lon")),
        check_vma=False,
    )
```

```python
import functools

import jax
import jax.numpy as jnp
from jax import lax
from jax.experimental import pallas as pl
from jax.experimental.pallas import tpu as pltpu
from jax.sharding import PartitionSpec as P

MESH = pl.DeviceIdType.MESH
BLOCK = 256
GROUPS = 4


def kernel(
    nlon, nlat,
    head, stor, east, north, leak, rech, rec, perm, crit, flags, ker, land,
    xo, po, do,
    HB, FL, S, E, N, K, Q, RC, PM, CR, M, U, R, W, FB, TH, TL, CH, CL, OUT, RX, DISP,
    scol, rcol, srow, rrow, snc, rnc, redA, redB,
    insem, outsem, hsend, hrecv, asend, arecv, bsend, brecv, dsend, drecv,
):
    L, rows, cols = HB.shape
    B = L - 1
    bands = rows // 8
    tile = cols // land.shape[1]
    width = ker.shape[1]
    lon, lat = lax.axis_index("lon"), lax.axis_index("lat")
    eastd = lax.rem(lon + 1, nlon)
    westd = lax.rem(lon + nlon - 1, nlon)
    northd = lax.rem(lat + 1, nlat)
    southd = lax.rem(lat + nlat - 1, nlat)
    mid = slice(128, 128 + cols)

    def fetch(sem, a, b):
        copy = pltpu.make_async_copy(a, b, insem.at[sem])
        copy.start()
        return copy

    group = rows // GROUPS
    early = [fetch(i, a, b) for i, (a, b) in enumerate(((head, HB), (flags, FL), (east, E.at[:, :, mid]), (north, N)))]
    grouped = []
    for g in range(GROUPS):
        rs = slice(g * group, (g + 1) * group)
        grouped.append([fetch(4 + 2 * g, leak.at[:, rs], K.at[:, rs]), fetch(5 + 2 * g, rech.at[:, rs], Q.at[:, rs])])
    late = [
        fetch(4 + 2 * GROUPS + i, a, b) for i, (a, b) in enumerate(((stor, S), (rec, RC), (perm, PM), (crit, CR)))
    ]

    barrier = pltpu.get_barrier_semaphore()
    for o in range(1, nlon):
        pl.semaphore_signal(barrier, inc=1, device_id={"lon": lax.rem(lon + o, nlon), "lat": lat}, device_id_type=MESH)
    for o in range(1, nlat):
        pl.semaphore_signal(barrier, inc=1, device_id={"lon": lon, "lat": lax.rem(lat + o, nlat)}, device_id_type=MESH)

    for ref in (U, R, W):
        for l in range(L):
            ref[l, 0:rows, 0:128] = jnp.zeros((rows, 128), jnp.float32)
            ref[l, 0:rows, cols + 128:cols + 256] = jnp.zeros((rows, 128), jnp.float32)
            ref[l, rows:rows + 8, mid] = jnp.zeros((8, cols), jnp.float32)
    for l in range(L):
        E[l, :, 0:128] = jnp.zeros((rows, 128), jnp.float32)

    sub = lax.broadcasted_iota(jnp.int32, (8, cols), 0)
    lane = lax.broadcasted_iota(jnp.int32, (rows, 128), 1)
    lane1 = lax.broadcasted_iota(jnp.int32, (1, 128), 1)

    spread = (
        lax.broadcasted_iota(jnp.int32, (land.shape[1], cols), 1) // tile
        == lax.broadcasted_iota(jnp.int32, (land.shape[1], cols), 0)
    )
    land_row = jnp.dot(
        jnp.broadcast_to(land[...].astype(jnp.float32), (8, land.shape[1])),
        spread.astype(jnp.float32),
        preferred_element_type=jnp.float32,
    )

    zero = jnp.zeros((8, 128), jnp.float32)

    def band(k):
        return pl.ds(pl.multiple_of(k * 8, 8), 8)

    early[0].wait()
    early[1].wait()

    @pl.loop(0, bands)
    def _(k):
        for l in range(L):
            m = land_row * FL[l, band(k), :].astype(jnp.float32)
            M[l, band(k), :] = m
            U[l, band(k), mid] = m * HB[l, band(k), :]

    def halo_copies(t):
        routes = [
            (scol.at[t, 0], rcol.at[t, 0], {"lon": eastd, "lat": lat}),
            (scol.at[t, 1], rcol.at[t, 1], {"lon": westd, "lat": lat}),
            (srow.at[t, 0], rrow.at[t, 0], {"lon": lon, "lat": northd}),
            (srow.at[t, 1], rrow.at[t, 1], {"lon": lon, "lat": southd}),
        ]
        if t == 0:
            routes.append((snc, rnc, {"lon": lon, "lat": northd}))
        return [
            pltpu.make_async_remote_copy(
                src_ref=s, dst_ref=d, send_sem=hsend.at[t, i], recv_sem=hrecv.at[t, i],
                device_id=to, device_id_type=MESH,
            )
            for i, (s, d, to) in enumerate(routes)
        ]

    def pack(t, ref):
        last = jnp.zeros((rows, 128), jnp.float32)
        first = jnp.zeros((rows, 128), jnp.float32)
        for l in range(L):
            tail = ref[l, 0:rows, cols:cols + 128]
            last = jnp.where(lane == l, pltpu.roll(tail, (l + 1) % 128, 1), last)
            start = ref[l, 0:rows, 128:256]
            first = jnp.where(lane == l, start if l == 0 else pltpu.roll(start, l, 1), first)
            srow[t, 0, l:l + 1, :] = ref[l, rows - 8:rows, mid][7:8, :]
            srow[t, 1, l:l + 1, :] = ref[l, 0:8, mid][0:1, :]
            if t == 0:
                tail = E[l, :, cols:cols + 128]
                last = jnp.where(lane == L + l, pltpu.roll(tail, (L + l + 1) % 128, 1), last)
                snc[l:l + 1, :] = N[l, rows - 8:rows, :][7:8, :]
        scol[t, 0] = last
        scol[t, 1] = first

    def send_halo(t, ref):
        pack(t, ref)
        if t == 0:
            pl.semaphore_wait(barrier, nlon - 1 + nlat - 1)
        copies = halo_copies(t)
        for c in copies:
            c.start()
        for l in range(L):
            if t == 0:
                FB[l] = jnp.zeros((8, cols), jnp.float32)
            else:
                FB[l] = -jnp.broadcast_to((rnc[l:l + 1, :] * has_south) * ref[l, 0:8, mid][0:1, :], (8, cols))
        return copies

    has_south = (lat > 0).astype(jnp.float32)
    has_north = (lat < nlat - 1).astype(jnp.float32)

    def take_halo(t, ref, copies, dst, shift, sign):
        for c in copies:
            c.wait()
        dot = jnp.zeros((8, 128), jnp.float32)

        def add(l, rs, c0, n, delta):
            at = (l, rs, slice(c0 + shift, c0 + shift + n))
            dst[at] = dst[at] + sign * (M[l, rs, c0:c0 + n] * delta)
            part = ref[l, rs, 128 + c0:128 + c0 + n] * delta
            total = zero
            for r in range(0, part.shape[0], 8):
                for c in range(0, n, 128):
                    total = total + part[r:r + 8, c:c + 128]
            return total

        whole, last = slice(0, rows), cols - 128
        for l in range(L):
            far = jnp.broadcast_to(rcol[t, 0][:, l:l + 1], (rows, 128))
            if t == 0:
                E[l, :, 0:128] = jnp.broadcast_to(rcol[0, 0][:, L + l:L + l + 1], (rows, 128))
                far = far - ref[l, 0:rows, 128:256]
            dot = dot + add(l, whole, 0, 128, jnp.where(lane == 0, -E[l, :, 0:128] * far, 0.0))
            far = jnp.broadcast_to(rcol[t, 1][:, l:l + 1], (rows, 128))
            dot = dot + add(l, whole, last, 128, jnp.where(lane == 127, -E[l, :, cols:cols + 128] * far, 0.0))
            far = jnp.broadcast_to(rrow[t, 0, l:l + 1, :] * has_south, (8, cols))
            if t == 0:
                far = far - ref[l, 0:8, mid]
            cond = jnp.broadcast_to(rnc[l:l + 1, :] * has_south, (8, cols))
            dot = dot + add(l, slice(0, 8), 0, cols, jnp.where(sub == 0, -cond * far, 0.0))
            far = jnp.broadcast_to(rrow[t, 1, l:l + 1, :] * has_north, (8, cols))
            dot = dot + add(l, slice(rows - 8, rows), 0, cols, jnp.where(sub == 7, -N[l, rows - 8:rows, :] * far, 0.0))
        return dot

    def divergence(ref, k):
        centre, out = [], []
        for l in range(L):
            u = ref[l, band(k), :]
            e = E[l, band(k), :]
            ue = pltpu.roll(u, cols + 255, 1)
            fe = e * (u[:, :cols + 128] - ue[:, :cols + 128])
            acc = fe[:, 128:] - pltpu.roll(fe, 1, 1)[:, 128:]
            uc = u[:, mid]
            nxt = ref[l, band(k + 1), mid]
            un = jnp.where(sub == 7, pltpu.roll(nxt, 7, 0), pltpu.roll(uc, 7, 0))
            fn = N[l, band(k), :] * (uc - un)
            rf = pltpu.roll(fn, 1, 0)
            acc = acc + fn - jnp.where(sub == 0, FB[l], rf)
            FB[l] = rf
            if l > 0:
                fv = K[l - 1, band(k), :] * (centre[l - 1] - uc)
                out[l - 1] = out[l - 1] + fv
                acc = acc - fv
            centre.append(uc)
            out.append(acc)
        return centre, out

    def fold(v):
        parts = [v[:, c:c + 128] for c in range(0, cols, 128)]
        while len(parts) > 1:
            parts = [sum(parts[i:i + 2][1:], parts[i]) for i in range(0, len(parts), 2)]
        return parts[0]

    def all_reduce(t, va, vb):
        a = jnp.sum(va, axis=0, keepdims=True)
        b = jnp.sum(vb, axis=0, keepdims=True)
        v = jnp.where(lane1 < 64, a + pltpu.roll(a, 64, 1), b + pltpu.roll(b, 64, 1))
        redA[t, lon] = v

        def lon_copy(o):
            return pltpu.make_async_remote_copy(
                src_ref=redA.at[t, lon], dst_ref=redA.at[t, lon], send_sem=asend.at[t, o], recv_sem=arecv.at[t, o],
                device_id={"lon": lax.rem(lon + o, nlon), "lat": lat}, device_id_type=MESH,
            )

        def lat_copy(o):
            return pltpu.make_async_remote_copy(
                src_ref=redB.at[t, lat], dst_ref=redB.at[t, lat], send_sem=bsend.at[t, o], recv_sem=brecv.at[t, o],
                device_id={"lon": lon, "lat": lax.rem(lat + o, nlat)}, device_id_type=MESH,
            )

        first = [lon_copy(o) for o in range(1, nlon)]
        second = [lat_copy(o) for o in range(1, nlat)]

        def start():
            for c in first:
                c.start()

        def middle():
            for c in first:
                c.wait()
            redB[t, lat] = jnp.sum(redA[t], axis=0)
            for c in second:
                c.start()

        def finish():
            for c in second:
                c.wait()
            total = jnp.sum(redB[t], axis=0)
            a = jnp.sum(jnp.where(lane1 < 64, total, 0.0), axis=1, keepdims=True)
            b = jnp.sum(jnp.where(lane1 < 64, 0.0, total), axis=1, keepdims=True)
            return a, b

        return start, middle, finish

    early[2].wait()
    early[3].wait()
    copies = send_halo(0, U)
    for g in range(GROUPS):
        for c in grouped[g]:
            c.wait()

        @pl.loop(g * bands // GROUPS, (g + 1) * bands // GROUPS)
        def _(k):
            _, out = divergence(U, k)
            for l in range(L):
                R[l, band(k), mid] = M[l, band(k), :] * (Q[l, band(k), :] - out[l])

    take_halo(0, U, copies, R, 128, -1.0)
    copies = send_halo(1, R)
    late[0].wait()

    def second(k, carry):
        a, b = carry
        centre, out = divergence(R, k)
        for l in range(L):
            r = centre[l]
            w = M[l, band(k), :] * (S[l, band(k), :] * r + out[l])
            W[l, band(k), mid] = w
            square = r * r if l == 0 else square + r * r
            cross = r * w if l == 0 else cross + r * w
        return a + fold(square), b + fold(cross)

    a, b = lax.fori_loop(0, bands, second, (zero, zero))
    b = b + take_halo(1, R, copies, W, 128, 1.0)
    start, middle, finish = all_reduce(0, a, b)
    start()
    copies = send_halo(2, W)

    @pl.loop(0, bands)
    def _(k):
        centre, out = divergence(W, k)
        for l in range(L):
            Q[l, band(k), :] = M[l, band(k), :] * (S[l, band(k), :] * centre[l] + out[l])

    middle()
    take_halo(2, W, copies, Q, 0, 1.0)
    rr0, bend = finish()
    alpha0 = rr0 / bend
    alpha_row = jnp.broadcast_to(alpha0, (8, 128))
    alpha_row = jnp.concatenate([alpha_row] * (cols // 128), axis=1)

    def third(k, carry):
        a, b = carry
        for l in range(L):
            w = W[l, band(k), mid]
            r1 = R[l, band(k), mid] - alpha_row * w
            s1 = w - alpha_row * Q[l, band(k), :]
            square = r1 * r1 if l == 0 else square + r1 * r1
            cross = r1 * s1 if l == 0 else cross + r1 * s1
        return a + fold(square), b + fold(cross)

    a, b = lax.fori_loop(0, bands, third, (zero, zero))
    start, middle, finish = all_reduce(1, a, b)
    start()

    half = width // 2
    h = half // BLOCK
    nb = cols // BLOCK
    lags = width // 128
    sides = BLOCK // 128

    def piece(b, e):
        if e < 0 or e >= lags:
            return jnp.zeros((1, 128), jnp.float32)
        return ker[b:b + 1, e * 128:(e + 1) * 128]

    for e in range(-1, lags + 2):
        places = [
            (d, ph, jh) for d in range(-h, h + 1) for ph in range(sides) for jh in range(sides)
            if sides * (d + h) + ph - jh == e
        ]
        for b in range(B):
            if 0 <= e <= lags:
                base = jnp.concatenate([piece(b, e), piece(b, e - 1)], axis=1)
                wide = pltpu.roll(jnp.broadcast_to(base, (128, 256)), 0, 1, stride=1, stride_axis=0)
                block = wide[:, :128].T
            else:
                block = jnp.zeros((128, 128), jnp.float32)
            hi = block.astype(jnp.bfloat16)
            lo = (block - hi.astype(jnp.float32)).astype(jnp.bfloat16)
            for d, ph, jh in places:
                at = (d + h, slice(b * BLOCK + ph * 128, b * BLOCK + ph * 128 + 128), slice(jh * 128, jh * 128 + 128))
                TH[at] = hi
                TL[at] = lo

    for c in late[1:]:
        c.wait()
    middle()
    rr1, curve = finish()
    beta = rr1 / rr0
    alpha1 = rr1 / (curve - beta * rr1 / alpha0)
    of_r = jnp.broadcast_to(alpha0 + alpha1 + alpha1 * beta, (16, BLOCK))
    of_w = jnp.broadcast_to(alpha1 * alpha0, (16, BLOCK))

    def compact(blocks):
        @pl.loop(0, rows // 16)
        def _(k):
            r = pl.ds(pl.multiple_of(k * 16, 16), 16)
            for p in blocks:
                cs = slice(p * BLOCK, (p + 1) * BLOCK)
                ps = slice(128 + p * BLOCK, 128 + (p + 1) * BLOCK)
                old = [HB[l, r, cs] for l in range(L)]
                new = [old[l] + of_r * R[l, r, ps] - of_w * W[l, r, ps] for l in range(L)]
                for l in range(L):
                    xo[l, r, cs] = new[l]
                for b in range(B):
                    both = M[b, r, cs] * M[b + 1, r, cs]
                    om = 0.5 * (old[b] + old[b + 1])
                    nm = 0.5 * (new[b] + new[b + 1])
                    cr = CR[b, r, cs]
                    over = jnp.maximum(cr - nm, 0.0)
                    comp = both * (RC[b, r, cs] * (om - nm) + PM[b, r, cs] * (over - jnp.maximum(cr - om, 0.0)))
                    po[b, r, cs] = cr - both * over
                    hi = comp.astype(jnp.bfloat16)
                    lo = (comp - hi.astype(jnp.float32)).astype(jnp.bfloat16)
                    dst = pl.ds(pl.multiple_of(p * rows + k * 16, 16), 16)
                    CH[dst, b * BLOCK:(b + 1) * BLOCK] = hi
                    CL[dst, b * BLOCK:(b + 1) * BLOCK] = lo

    edge = [p for p in range(nb) if p < h or p >= nb - h]
    compact(edge)

    def product(d, low, high):
        ch, cl = CH[low * rows:high * rows, :], CL[low * rows:high * rows, :]
        th, tl = TH[d + h], TL[d + h]
        dot = functools.partial(jnp.dot, preferred_element_type=jnp.float32)
        return dot(ch, th) + (dot(ch, tl) + dot(cl, th))

    for d in range(h, 0, -1):
        left = product(d, 0, d)
        right = product(-d, nb - d, nb)
        at = slice((h - d) * rows, h * rows)
        end = slice((h + nb) * rows, (h + nb + d) * rows)
        if d == h:
            OUT[at, :] = left
            OUT[end, :] = right
        else:
            OUT[at, :] += left
            OUT[end, :] += right
    exts = [
        pltpu.make_async_remote_copy(
            src_ref=OUT.at[0:h * rows, :], dst_ref=RX.at[1], send_sem=dsend.at[0], recv_sem=drecv.at[0],
            device_id={"lon": westd, "lat": lat}, device_id_type=MESH,
        ),
        pltpu.make_async_remote_copy(
            src_ref=OUT.at[(h + nb) * rows:(2 * h + nb) * rows, :], dst_ref=RX.at[0], send_sem=dsend.at[1], recv_sem=drecv.at[1],
            device_id={"lon": eastd, "lat": lat}, device_id_type=MESH,
        ),
    ]
    for c in exts:
        c.start()
    compact([p for p in range(nb) if p not in edge])
    OUT[h * rows:(h + nb) * rows, :] = product(0, 0, nb)
    for d in range(1, h + 1):
        OUT[h * rows:(h + nb - d) * rows, :] += product(d, d, nb)
        OUT[(h + d) * rows:(h + nb) * rows, :] += product(-d, 0, nb - d)
    for c in exts:
        c.wait()
    for p in range(nb):
        v = OUT[(h + p) * rows:(h + p + 1) * rows, :]
        if p < h:
            v = v + RX[0, p * rows:(p + 1) * rows, :]
        if p >= nb - h:
            q = p - (nb - h)
            v = v + RX[1, q * rows:(q + 1) * rows, :]
        do[:, p * BLOCK:(p + 1) * BLOCK] = v


def per_device(
    nlon, nlat, head, storage, east_cond, north_cond, leakance, recharge,
    recoverable_skeleton_coefs, permanent_skeleton_coefs, critical_heads, kernel_, land_tiles, cell_flags,
):
    L, rows, cols = head.shape
    B = L - 1
    width = kernel_.shape[1]
    f32 = jnp.float32
    full, inter = (L, rows, cols), (B, rows, cols)
    padded = (L, rows + 8, cols + 256)
    h = width // 2 // BLOCK
    nb = cols // BLOCK
    V = pltpu.VMEM
    dma = pltpu.SemaphoreType.DMA
    scratch = [
        V(full, f32), V(full, jnp.int32), V(full, f32), V((L, rows, cols + 128), f32), V(full, f32), V(inter, f32),
        V(full, f32), V(inter, f32), V(inter, f32), V(inter, f32), V(full, f32),
        V(padded, f32), V(padded, f32), V(padded, f32), V((L, 8, cols), f32),
        V((2 * h + 1, B * BLOCK, BLOCK), jnp.bfloat16), V((2 * h + 1, B * BLOCK, BLOCK), jnp.bfloat16),
        V((nb * rows, B * BLOCK), jnp.bfloat16), V((nb * rows, B * BLOCK), jnp.bfloat16),
        V(((nb + 2 * h) * rows, BLOCK), f32), V((2, h * rows, BLOCK), f32), V((rows, cols), f32),
        V((3, 2, rows, 128), f32), V((3, 2, rows, 128), f32),
        V((3, 2, L, cols), f32), V((3, 2, L, cols), f32), V((L, cols), f32), V((L, cols), f32),
        V((2, nlon, 1, 128), f32), V((2, nlat, 1, 128), f32),
        dma((8 + 2 * GROUPS,)), dma((3,)), dma((3, 5)), dma((3, 5)), dma((2, nlon)), dma((2, nlon)), dma((2, nlat)), dma((2, nlat)),
        dma((2,)), dma((2,)),
    ]
    hbm = pl.BlockSpec(memory_space=pl.ANY)
    vmem = pl.BlockSpec(memory_space=pltpu.VMEM)
    outs = pl.pallas_call(
        functools.partial(kernel, nlon, nlat),
        out_shape=(
            V(full, f32), V(inter, f32), V((rows, cols), f32),
        ),
        in_specs=[hbm] * 10 + [vmem] * 2,
        out_specs=(vmem,) * 3,
        scratch_shapes=scratch,
        name="aquifer_step",
        compiler_params=pltpu.CompilerParams(collective_id=0, has_side_effects=True, vmem_limit_bytes=52 * 1024 * 1024),
    )(
        head, storage, east_cond, north_cond, leakance, recharge, recoverable_skeleton_coefs,
        permanent_skeleton_coefs, critical_heads, cell_flags, kernel_, land_tiles,
    )

    def put(a, b, c, x, y, z, sem):
        copies = [pltpu.make_async_copy(s, d, sem.at[i]) for i, (s, d) in enumerate(((a, x), (b, y), (c, z)))]
        for copy in copies:
            copy.start()
        for copy in copies:
            copy.wait()

    return pl.pallas_call(
        put,
        out_shape=(
            jax.ShapeDtypeStruct(full, f32), jax.ShapeDtypeStruct(inter, f32), jax.ShapeDtypeStruct((rows, cols), f32),
        ),
        in_specs=[vmem] * 3,
        out_specs=(hbm,) * 3,
        scratch_shapes=[dma((3,))],
        name="put",
        compiler_params=pltpu.CompilerParams(vmem_limit_bytes=1024 * 1024),
    )(*outs)


def solution(mesh):
    block = P(None, "lat", "lon")
    placed = (block,) * 9 + (P(), P("lat", "lon"), block)
    return jax.shard_map(
        functools.partial(per_device, mesh.shape["lon"], mesh.shape["lat"]),
        mesh=mesh,
        in_specs=placed,
        out_specs=(block, block, P("lat", "lon")),
        check_vma=False,
    )
```
